32 devices in a mesh: section: 4 (over y, core), expert: 8 (over z, x).
Axes of the slice: x: 2, y: 2, z: 4, core: 2. Of those that a mesh axis runs over, the one named last changes fastest.
Arguments:
- states: bfloat16 [4, 64, 3584], P('section', 'expert'), may hold values from -6 to 6
- norm_gain: float32 [4, 3584], P('section'), may hold values from 0.1 to 1.9
- router: bfloat16 [4, 3584, 4], P('section'), may hold values from -0.09375 to 0.09375
- w_gate: bfloat16 [4, 3584, 4096], P('section', None, 'expert'), may hold values from -0.09375 to 0.09375
- w_up: bfloat16 [4, 3584, 4096], P('section', None, 'expert'), may hold values from -0.09375 to 0.09375
- w_down: bfloat16 [4, 4096, 3584], P('section', 'expert'), may hold values from -0.1875 to 0.1875
- routes: int32 [2, 4, 64, 2], P(None, 'section', 'expert'), may hold values from 0 to 3, all different within a row; in each aligned block of 8 rows (0 to 7, 8 to 15, ..., all dimensions but the last counted through in order) at most 8 rows name the same one
Outputs:
- final_states: bfloat16 [4, 64, 3584], P('section', 'expert')
The draws below stay inside these ranges and needn't reach their ends.
Inputs may be any that keep to these rules, and one draw needn't show every extreme that they name: `routes`: each token names 2 different experts. Within one tick and one section, among the 8 tokens of one index of the expert axis, no expert is named by more than 8 tokens; in some such blocks one expert is named by exactly 8.
All inputs are finite; a program needn't handle non-finite values.
Results may differ from the reference program's by a relative error of at most 0.0064.
Values may be sent and summed in bfloat16 or wider, within the bound.
No kernel may reach another device: no remote copies, remote signals or barrier semaphores. Data moves between devices by JAX's collectives and lax.ppermute only.
A program may use at most 64 MiB of HBM per device.

```python
import math
import jax
import jax.numpy as jnp
import numpy as np
from jax import lax

D = 3584
FF = 1024
EXPERTS = 4
TOPK = 2
TICKS = 2
TOK_DEV = 8
SHARDS = 2
HID_DEV = 512
CAP = 8
SECTIONS = 4
TOKS = 64
N_EXPERT = 8


def levels(stream_key, extent, cuts, least, high):
    level = 1.0
    for dim, blocks in cuts:
        heights = jax.random.uniform(jax.random.fold_in(jax.random.fold_in(stream_key, 6), dim), (blocks,), jnp.float32, least / len(cuts), high / len(cuts))
        level = level * jnp.repeat(jnp.exp(heights), extent[dim] // blocks).reshape((-1,) + (1,) * (len(extent) - 1 - dim))
    return level


def shared_out(rng, own, number, rows, count, top, most, skew):
    order = jax.random.permutation(rng, count)
    packed, ordinary = load_shares(count, rows * top, most, skew, True), load_shares(count, rows * top, most, skew, False)
    places = jnp.arange(count)

    def named(lengths, offset_by):
        used = int((lengths > 0).sum())
        fixed = max(1, used // 4)
        moved = fixed + (places - fixed + offset_by * (used - fixed)) % max(1, count - fixed)
        return jnp.zeros((count,), jnp.int32).at[order[jnp.where(places < fixed, places, moved)]].set(jnp.asarray(lengths, jnp.int32))

    lengths = jnp.where(number % 4 == 0, named(packed, number // 4), named(ordinary, number - number // 4 - 1))
    mixed = jax.random.permutation(jax.random.fold_in(own, 3), count)
    donor, sink = mixed[0:count // 2 * 2:2], mixed[1:count // 2 * 2:2]
    room = jnp.minimum(lengths[donor] - 1, most - lengths[sink]) // 2
    room = jnp.where((donor == order[0]) | (sink == order[0]) | (lengths[sink] == 0), 0, jnp.maximum(room, 0))
    moved = jax.random.randint(jax.random.fold_in(own, 4), (count // 2,), 0, 1 << 20) % (room + 1)
    lengths = lengths.at[donor].add(-moved).at[sink].add(moved)
    items = jnp.searchsorted(jnp.cumsum(lengths), jnp.arange(rows * top), side="right").astype(jnp.int32)
    listing = items.reshape(top, rows).T
    listing = listing[jax.random.permutation(jax.random.fold_in(own, 1), rows)]
    offset_by = jax.random.randint(jax.random.fold_in(own, 2), (rows, 1), 0, top)
    return jnp.take_along_axis(listing, (jnp.arange(top)[None, :] + offset_by) % top, axis=1)


def load_shares(count, total, reach, lean, full):
    portions = [(1 << 20) // math.isqrt(grade ** lean) + 1 for grade in range(1, count + 1)]
    largest = reach if full else min(reach, max(-(-total // count), total * portions[0] // sum(portions)))
    least = 1 if total - largest >= count - 1 else 0
    given, spare = [largest] + [least] * (count - 1), total - largest - least * (count - 1)
    while spare > 0:
        movable = [i for i in range(1, count) if given[i] < largest] or [i for i in range(1, count) if given[i] < reach]
        mass, remaining = sum([portions[i] for i in movable]), spare
        for i in movable:
            extra = min(reach - given[i], max(1, remaining * portions[i] // mass), spare)
            given[i] = given[i] + extra
            spare = spare - extra
    return np.array(given)


def scatter_about(rng, shape, scale, limit, cuts=(), held_as=jnp.bfloat16):
    level = levels(rng, shape, cuts, -0.22, 0.18) if cuts else 1.0
    values = jax.random.normal(rng, shape, jnp.float32) * scale * level
    return jnp.minimum(jnp.maximum(values, -limit), limit).astype(held_as)


def setup_inputs(seed: int = 0) -> dict:
    key_of = jax.random.split(jax.random.key(seed), 8)
    states = scatter_about(key_of[0], (SECTIONS, TOKS, D), 1.0, 6.0, ((0, 4), (1, 8)))
    norm_gain = jnp.clip(1.0 + 0.18 * jax.random.normal(key_of[1], (SECTIONS, D), jnp.float32), 0.1, 1.9)
    router = scatter_about(key_of[2], (SECTIONS, D, EXPERTS), D ** -0.5, 0.09375, ((0, 4),))
    w_gate = scatter_about(key_of[3], (SECTIONS, D, EXPERTS * FF), D ** -0.5, 0.09375, ((0, 4), (2, 8)))
    w_up = scatter_about(key_of[4], (SECTIONS, D, EXPERTS * FF), D ** -0.5, 0.09375, ((0, 4), (2, 8)))
    w_down = scatter_about(key_of[5], (SECTIONS, EXPERTS * FF, D), FF ** -0.5, 0.1875, ((0, 4), (1, 8)))
    routes_keys = jax.random.split(jax.random.fold_in(key_of[6], 1), TICKS * SECTIONS * TOKS // TOK_DEV)
    routes_turns = jax.random.permutation(jax.random.fold_in(key_of[6], 3), TICKS * SECTIONS * TOKS // TOK_DEV)
    routes = jax.vmap(lambda own, number: shared_out(jax.random.fold_in(key_of[6], 2), own, number, TOK_DEV, EXPERTS, TOPK, CAP, 2))(routes_keys, routes_turns).reshape((TICKS, SECTIONS, TOKS, TOPK))
    return dict(states=states, norm_gain=norm_gain, router=router, w_gate=w_gate, w_up=w_up, w_down=w_down, routes=routes)


EPSILON = 1e-06

def normalize(states, gain):
    values = states.astype(jnp.float32)
    meansq = lax.optimization_barrier(jnp.mean(values * values, axis=-1, keepdims=True))
    return (values * lax.rsqrt(meansq + EPSILON) * gain).astype(jnp.bfloat16)

def slot_positions(expert_ids, experts, sources):
    onehot = (expert_ids[:, :, None] == jnp.arange(experts, dtype=jnp.int32)).astype(jnp.int32)
    named = lax.optimization_barrier(jnp.sum(onehot, axis=1))
    grouped = named.reshape(sources, -1, experts)
    before = (jnp.cumsum(grouped, axis=1) - grouped).reshape(-1, experts)
    position = lax.optimization_barrier(jnp.sum(onehot * before[:, None, :], axis=2))
    return (onehot, position)

def gate_values(normed, router, onehot):
    logits = jnp.dot(normed, router, preferred_element_type=jnp.float32)
    affinity = jax.nn.sigmoid(logits)
    chosen = lax.optimization_barrier(jnp.sum(onehot.astype(jnp.float32) * affinity[:, None, :], axis=2))
    return chosen / lax.optimization_barrier(jnp.sum(chosen, axis=1, keepdims=True))

def layer(states, gain, router, w_gate, w_up, w_down, expert_ids):
    normed = normalize(states, gain)
    onehot, position = slot_positions(expert_ids, EXPERTS, N_EXPERT)
    gates = gate_values(normed, router, onehot)
    source = (jnp.arange(TOKS, dtype=jnp.int32) // TOK_DEV)[:, None]
    column = source * CAP + position
    buffers = jnp.zeros((EXPERTS, N_EXPERT * CAP, D), jnp.bfloat16)
    spread_rows = jnp.broadcast_to(normed[:, None, :], (TOKS, TOPK, D))
    buffers = buffers.at[expert_ids, column].set(spread_rows)
    inputs = buffers.astype(jnp.float32)
    gate_matrix = w_gate.astype(jnp.float32).reshape(D, EXPERTS, FF)
    lift_matrix = w_up.astype(jnp.float32).reshape(D, EXPERTS, FF)
    gate_out = jnp.einsum('erd,def->erf', inputs, gate_matrix)
    lifted = jnp.einsum('erd,def->erf', inputs, lift_matrix)
    hidden = (jax.nn.silu(gate_out) * lifted).astype(jnp.bfloat16)
    pieces = hidden.astype(jnp.float32).reshape(EXPERTS, N_EXPERT * CAP, SHARDS, HID_DEV)
    down_matrix = w_down.astype(jnp.float32).reshape(EXPERTS, SHARDS, HID_DEV, D)
    partial_value = jnp.einsum('ersh,eshd->ersd', pieces, down_matrix).astype(jnp.bfloat16)
    partial_value = lax.optimization_barrier(partial_value)
    expert_out = lax.optimization_barrier(jnp.sum(partial_value.astype(jnp.float32), axis=2))
    picked = expert_out[expert_ids, column]
    mixed = lax.optimization_barrier(jnp.sum(picked * gates[:, :, None], axis=1))
    return (states.astype(jnp.float32) + mixed).astype(jnp.bfloat16)

def one_section(operands):
    return layer(*operands)

def reference(states, norm_gain, router, w_gate, w_up, w_down, routes):
    for tick_index in range(TICKS):
        updated = lax.map(one_section, (states, norm_gain, router, w_gate, w_up, w_down, routes[tick_index]))
        states = jnp.roll(updated, 1, axis=0)
    return states
```

```python
import functools

import jax
import jax.numpy as jnp
from jax import lax
from jax.experimental import pallas as pl
from jax.experimental.pallas import tpu as pltpu
from jax.sharding import PartitionSpec as P

TICKS = 2
EPSILON = 1e-06
AXES = ("section", "expert")
LANES = 128


def relayed(value, sections, experts, shards, hop, expert_bits, shard_bits):
    devices = experts * shards
    pairs = []
    for s in range(sections):
        for e in range(experts):
            for h in range(shards):
                target = (e ^ expert_bits) * shards + (h ^ shard_bits)
                pairs.append((s * devices + e * shards + h, (s + hop) % sections * devices + target))
    return lax.ppermute(value, AXES, pairs)


def fetch_kernel(gate_ref, lift_ref, down_ref, gate_out, lift_out, down_out, sems):
    copies = [
        pltpu.make_async_copy(source, target, sems.at[i])
        for i, (source, target) in enumerate(
            ((gate_ref, gate_out), (lift_ref, lift_out), (down_ref, down_out))
        )
    ]
    for copy in copies:
        copy.start()
    for copy in copies:
        copy.wait()


def fetched(gate, lift, down):
    return pl.pallas_call(
        fetch_kernel,
        out_shape=tuple(pltpu.VMEM(w.shape, w.dtype) for w in (gate, lift, down)),
        in_specs=[pl.BlockSpec(memory_space=pl.ANY)] * 3,
        out_specs=[pl.BlockSpec(memory_space=pltpu.VMEM)] * 3,
        scratch_shapes=[pltpu.SemaphoreType.DMA((3,))],
        compiler_params=pltpu.CompilerParams(vmem_limit_bytes=1 << 20),
        name="fetch",
    )(gate, lift, down)


def expert_kernel(count, shards, *refs):
    blocks = refs[:count]
    named_ref, mine_ref, gain_ref, router_ref, gate_ref, lift_ref, down_ref = refs[count : count + 7]
    outs = refs[count + 7 : count + 7 + shards]
    normed_ref = refs[count + 7 + shards]
    rows = blocks[0].shape[0]
    gain = gain_ref[...]
    for pair in range(0, count, 2):
        parts = []
        for block in blocks[pair : pair + 2]:
            values = block[...].astype(jnp.float32)
            meansq = jnp.mean(values * values, axis=-1, keepdims=True)
            parts.append(values * lax.rsqrt(meansq + EPSILON) * gain)
        normed_ref[pl.ds(pair * rows, 2 * rows), :] = jnp.concatenate(parts, axis=0).astype(jnp.bfloat16)
    normed = normed_ref[...]
    logits = lax.dot_general(
        normed, router_ref[...], (((1,), (1,)), ((), ())), preferred_element_type=jnp.float32
    )
    experts = router_ref.shape[0]
    chosen = jax.nn.sigmoid(logits) * named_ref[...][:, :experts]
    scale = jnp.sum(chosen * mine_ref[...][:, :experts], axis=1, keepdims=True) / jnp.sum(
        chosen, axis=1, keepdims=True
    )
    gate_out = jnp.dot(normed, gate_ref[...], preferred_element_type=jnp.float32)
    lifted = jnp.dot(normed, lift_ref[...], preferred_element_type=jnp.float32)
    hidden = (gate_out / (1.0 + jnp.exp(-gate_out)) * lifted).astype(jnp.bfloat16)
    partial_value = jnp.dot(hidden, down_ref[...], preferred_element_type=jnp.float32)
    partial_value = (partial_value * scale).astype(jnp.bfloat16)
    share = partial_value.shape[0] // shards
    for i, out in enumerate(outs):
        out[...] = partial_value[i * share : (i + 1) * share]


def expert_parts(blocks, named, mine, gain, router, gate, lift, down, shards):
    count = len(blocks)
    rows, width = blocks[0].shape
    return pl.pallas_call(
        functools.partial(expert_kernel, count, shards),
        out_shape=tuple(
            jax.ShapeDtypeStruct((count // shards * rows, width), jnp.bfloat16) for _ in range(shards)
        ),
        in_specs=[pl.BlockSpec(memory_space=pltpu.VMEM)] * (count + 7),
        out_specs=[pl.BlockSpec(memory_space=pltpu.VMEM)] * shards,
        scratch_shapes=[pltpu.VMEM((count * rows, width), jnp.bfloat16)],
        compiler_params=pltpu.CompilerParams(vmem_limit_bytes=24 << 20),
        name="experts",
    )(*blocks, named, mine, gain, router, gate, lift, down)


def on_device(states, norm_gain, router, w_gate, w_up, w_down, routes):
    sections = lax.axis_size("section")
    devices = lax.axis_size("expert")
    experts = router.shape[2]
    shards = devices // experts
    send = functools.partial(relayed, sections=sections, experts=experts, shards=shards)

    def gathered(own):
        line = [own] + [send(own, hop=0, expert_bits=k, shard_bits=0) for k in range(1, experts)]
        blocks = list(line)
        for j in range(1, shards):
            blocks += [send(block, hop=0, expert_bits=0, shard_bits=j) for block in line]
        return blocks

    current = states[0]
    rows = current.shape[0]
    ids = jnp.arange(experts, dtype=jnp.int32)
    named = jnp.sum((routes[:, 0, :, :, None] == ids).astype(jnp.float32), axis=2)
    named = jnp.pad(jnp.moveaxis(named, 0, 1).reshape(rows, TICKS * experts), ((0, 0), (0, LANES - TICKS * experts)))
    mine = (jnp.arange(LANES, dtype=jnp.int32) == lax.axis_index("expert") // shards).astype(jnp.float32)[None]

    weights = None
    table = None
    for tick in range(TICKS):
        blocks = gathered(current)
        residual = send(current, hop=1, expert_bits=0, shard_bits=0)
        if tick == 0:
            line = jnp.concatenate(
                [named] + [send(named, hop=0, expert_bits=k, shard_bits=0) for k in range(1, experts)]
            )
            table = jnp.concatenate(
                [line] + [send(line, hop=0, expert_bits=0, shard_bits=j) for j in range(1, shards)]
            )
            weights = fetched(w_gate[0], w_up[0], w_down[0])
        parts = expert_parts(
            blocks,
            table[:, tick * experts : (tick + 1) * experts],
            mine[:, :experts],
            norm_gain,
            router[0].T,
            *weights,
            shards,
        )
        arrived = [
            send(part, hop=1, expert_bits=0, shard_bits=j).astype(jnp.float32) for j, part in enumerate(parts)
        ]
        summed = sum(arrived[1:], arrived[0]).reshape(experts, rows, -1)
        total = residual.astype(jnp.float32) + summed[0]
        for k in range(1, experts):
            total = total + send(
                summed[k].astype(jnp.bfloat16), hop=0, expert_bits=k, shard_bits=0
            ).astype(jnp.float32)
        current = total.astype(jnp.bfloat16)
    return current[None]


def solution(mesh):
    placed = (
        P("section", "expert", None),
        P("section", None),
        P("section", None, None),
        P("section", None, "expert"),
        P("section", None, "expert"),
        P("section", "expert", None),
        P(None, "section", "expert", None),
    )
    return jax.shard_map(
        on_device,
        mesh=mesh,
        in_specs=placed,
        out_specs=P("section", "expert", None),
        check_vma=False,
    )
```

```python
import functools

import jax
import jax.numpy as jnp
from jax import lax
from jax.experimental import pallas as pl
from jax.experimental.pallas import tpu as pltpu
from jax.sharding import PartitionSpec as P


TICKS = 2
EPSILON = 1e-06
AXES = ("section", "expert")
LANES = 128
PIECES = 3
FETCHES = 4
VMEM_BYTES = 64 << 20


def relayed(value, sections, experts, shards, hop, expert_bits, shard_bits):
    devices = experts * shards
    pairs = []
    for s in range(sections):
        for e in range(experts):
            for h in range(shards):
                target = (e ^ expert_bits) * shards + (h ^ shard_bits)
                pairs.append((s * devices + e * shards + h, (s + hop) % sections * devices + target))
    return lax.ppermute(value, AXES, pairs)


def fetch_kernel(count, *refs):
    copies = []
    for i in range(count):
        source, target = refs[i], refs[count + i]
        step = source.shape[0] // FETCHES
        for part in range(FETCHES):
            span = pl.ds(part * step, step)
            copies.append(
                pltpu.make_async_copy(source.at[span], target.at[span], refs[2 * count].at[i * FETCHES + part])
            )
    for copy in copies:
        copy.start()
    for copy in copies:
        copy.wait()


def fetched(*weights):
    count = len(weights)
    held = sum(w.size * w.dtype.itemsize for w in weights)
    return pl.pallas_call(
        functools.partial(fetch_kernel, count),
        out_shape=tuple(pltpu.VMEM(w.shape, w.dtype) for w in weights),
        in_specs=[pl.BlockSpec(memory_space=pl.ANY)] * count,
        out_specs=[pl.BlockSpec(memory_space=pltpu.VMEM)] * count,
        scratch_shapes=[pltpu.SemaphoreType.DMA((count * FETCHES,))],
        compiler_params=pltpu.CompilerParams(vmem_limit_bytes=VMEM_BYTES - held - held // 5),
    )(*weights)


def share_kernel(own_ref, ids_ref, home_ref, gain_ref, router_ref, out_ref):
    rows, width = own_ref.shape
    experts = router_ref.shape[0]
    values = own_ref[...].astype(jnp.float32)
    meansq = jnp.mean(values * values, axis=-1, keepdims=True)
    normed = (values * lax.rsqrt(meansq + EPSILON) * gain_ref[...]).astype(jnp.bfloat16)
    logits = lax.dot_general(
        normed, router_ref[...], (((1,), (1,)), ((), ())), preferred_element_type=jnp.float32
    )
    affinity = jax.nn.sigmoid(logits)
    column = lax.broadcasted_iota(jnp.int32, (rows, experts), 1)
    named = jnp.zeros((rows, experts), jnp.bool_)
    for k in range(ids_ref.shape[1]):
        named = named | (ids_ref[:, k : k + 1] == column)
    chosen = jnp.where(named, affinity, 0.0)
    gates = chosen / jnp.sum(chosen, axis=1, keepdims=True)
    lane = lax.broadcasted_iota(jnp.int32, (rows, LANES), 1)
    extra = jnp.zeros((rows, LANES), jnp.float32)
    for k in range(experts):
        rest = jnp.sum(jnp.where(column == (home_ref[0] ^ k), gates, 0.0), axis=1, keepdims=True)
        for piece in range(PIECES):
            top = rest.astype(jnp.bfloat16).astype(jnp.float32)
            extra = jnp.where(lane == k * PIECES + piece, top, extra)
            rest = rest - top
    out_ref[:, :width] = own_ref[...]
    out_ref[:, width:] = extra.astype(jnp.bfloat16)


def with_shares(own, expert_ids, home, gain, router):
    rows, width = own.shape
    vmem = pl.BlockSpec(memory_space=pltpu.VMEM)
    return pl.pallas_call(
        share_kernel,
        out_shape=jax.ShapeDtypeStruct((rows, width + LANES), jnp.bfloat16),
        in_specs=[vmem, vmem, pl.BlockSpec(memory_space=pltpu.SMEM), vmem, vmem],
        out_specs=vmem,
        compiler_params=pltpu.CompilerParams(vmem_limit_bytes=4 << 20),
        name="shares",
    )(own, expert_ids, home, gain, router)


def fold_kernel(shards, *refs):
    outs = refs[shards:]
    rows = outs[0].shape[0]
    for k, out in enumerate(outs):
        span = pl.ds(k * rows, rows)
        total = refs[0][span, :].astype(jnp.float32)
        for part in refs[1:shards]:
            total = total + part[span, :].astype(jnp.float32)
        out[...] = total.astype(out.dtype)


def folded(parts, experts):
    rows, width = parts[0].shape[0] // experts, parts[0].shape[1]
    vmem = pl.BlockSpec(memory_space=pltpu.VMEM)
    return pl.pallas_call(
        functools.partial(fold_kernel, len(parts)),
        out_shape=tuple(
            jax.ShapeDtypeStruct((rows, width), jnp.float32 if k == 0 else jnp.bfloat16) for k in range(experts)
        ),
        in_specs=[vmem] * len(parts),
        out_specs=[vmem] * experts,
        compiler_params=pltpu.CompilerParams(vmem_limit_bytes=4 << 20),
        name="fold",
    )(*parts)


def finish_kernel(count, shared_ref, *refs):
    out_ref = refs[count]
    width = out_ref.shape[1]
    total = shared_ref[:, :width].astype(jnp.float32)
    extra = shared_ref[:, width:].astype(jnp.float32)
    lane = lax.broadcasted_iota(jnp.int32, extra.shape, 1)
    for k in range(count):
        terms = jnp.where((lane >= k * PIECES) & (lane < (k + 1) * PIECES), extra, 0.0)
        total = total + jnp.sum(terms, axis=1, keepdims=True) * refs[k][...].astype(jnp.float32)
    out_ref[...] = total.astype(jnp.bfloat16)


def finished(shared, pieces):
    rows, width = pieces[0].shape
    vmem = pl.BlockSpec(memory_space=pltpu.VMEM)
    return pl.pallas_call(
        functools.partial(finish_kernel, len(pieces)),
        out_shape=jax.ShapeDtypeStruct((rows, width), jnp.bfloat16),
        in_specs=[vmem] * (1 + len(pieces)),
        out_specs=vmem,
        compiler_params=pltpu.CompilerParams(vmem_limit_bytes=4 << 20),
        name="finish",
    )(shared, *pieces)


def expert_kernel(count, shards, *refs):
    blocks = refs[:count]
    gain_ref, gate_ref, lift_ref, down_ref = refs[count : count + 4]
    outs = refs[count + 4 : count + 4 + shards]
    normed_ref = refs[count + 4 + shards]
    rows = blocks[0].shape[0]
    gain = gain_ref[...]
    for pair in range(0, count, 2):
        parts = []
        for block in blocks[pair : pair + 2]:
            values = block[...].astype(jnp.float32)
            meansq = jnp.mean(values * values, axis=-1, keepdims=True)
            parts.append(values * lax.rsqrt(meansq + EPSILON) * gain)
        normed_ref[pl.ds(pair * rows, 2 * rows), :] = jnp.concatenate(parts, axis=0).astype(jnp.bfloat16)
    normed = normed_ref[...]
    gate_out = jnp.dot(normed, gate_ref[...], preferred_element_type=jnp.float32)
    lifted = jnp.dot(normed, lift_ref[...], preferred_element_type=jnp.float32)
    hidden = (gate_out / (1.0 + jnp.exp(-gate_out)) * lifted).astype(jnp.bfloat16)
    partial_value = jnp.dot(hidden, down_ref[...], preferred_element_type=jnp.float32).astype(jnp.bfloat16)
    share = partial_value.shape[0] // shards
    for i, out in enumerate(outs):
        out[...] = partial_value[i * share : (i + 1) * share]


def expert_parts(blocks, gain, gate, lift, down, shards):
    count = len(blocks)
    rows, width = blocks[0].shape
    return pl.pallas_call(
        functools.partial(expert_kernel, count, shards),
        out_shape=tuple(
            jax.ShapeDtypeStruct((count // shards * rows, width), jnp.bfloat16) for _ in range(shards)
        ),
        in_specs=[pl.BlockSpec(memory_space=pltpu.VMEM)] * (count + 4),
        out_specs=[pl.BlockSpec(memory_space=pltpu.VMEM)] * shards,
        scratch_shapes=[pltpu.VMEM((count * rows, width), jnp.bfloat16)],
        compiler_params=pltpu.CompilerParams(vmem_limit_bytes=8 << 20),
        name="experts",
    )(*blocks, gain, gate, lift, down)


def on_device(states, norm_gain, router, w_gate, w_up, w_down, routes):
    sections = lax.axis_size("section")
    devices = lax.axis_size("expert")
    experts = router.shape[2]
    shards = devices // experts
    send = functools.partial(relayed, sections=sections, experts=experts, shards=shards)
    far_first = range(experts - 1, 0, -1)

    def gathered(own):
        line = {0: own}
        for k in far_first:
            line[k] = send(own, hop=0, expert_bits=k, shard_bits=0)
        blocks = {(0, k): line[k] for k in range(experts)}
        for k in range(experts):
            for j in range(1, shards):
                blocks[j, k] = send(line[k], hop=0, expert_bits=0, shard_bits=j)
        return [blocks[j, k] for j in range(shards) for k in range(experts)]

    current = states[0]
    home = (lax.axis_index("expert") // shards).astype(jnp.int32)[None]
    for tick in range(TICKS):
        blocks = gathered(current)
        weights = fetched(w_gate[0], w_up[0], w_down[0])
        shared = with_shares(current, routes[tick, 0], home, norm_gain, router[0].T)
        shared = send(shared, hop=1, expert_bits=0, shard_bits=0)
        parts = expert_parts(blocks, norm_gain, *weights, shards)
        sums = folded([send(part, hop=1, expert_bits=0, shard_bits=j) for j, part in enumerate(parts)], experts)
        pieces = {0: sums[0]}
        for k in far_first:
            pieces[k] = send(sums[k], hop=0, expert_bits=k, shard_bits=0)
        current = finished(shared, [pieces[k] for k in range(experts)])
    return current[None]


def solution(mesh):
    placed = (
        P("section", "expert", None),
        P("section", None),
        P("section", None, None),
        P("section", None, "expert"),
        P("section", None, "expert"),
        P("section", "expert", None),
        P(None, "section", "expert", None),
    )
    return jax.shard_map(
        on_device,
        mesh=mesh,
        in_specs=placed,
        out_specs=P("section", "expert", None),
        check_vma=False,
    )
```

```python
import functools

import jax
import jax.numpy as jnp
from jax import lax
from jax.experimental import pallas as pl
from jax.experimental.pallas import tpu as pltpu
from jax.sharding import PartitionSpec as P


TICKS = 2
EPSILON = 1e-06
AXES = ("section", "expert")
LANES = 128
PIECES = 3
FETCHES = 4
VMEM_BYTES = 64 << 20


def relayed(value, sections, experts, shards, hop, expert_bits, shard_bits):
    devices = experts * shards
    pairs = []
    for s in range(sections):
        for e in range(experts):
            for h in range(shards):
                target = (e ^ expert_bits) * shards + (h ^ shard_bits)
                pairs.append((s * devices + e * shards + h, (s + hop) % sections * devices + target))
    return lax.ppermute(value, AXES, pairs)


def fetch_kernel(count, *refs):
    copies = []
    for i in range(count):
        source, target = refs[i], refs[count + i]
        step = source.shape[0] // FETCHES
        for part in range(FETCHES):
            span = pl.ds(part * step, step)
            copies.append(
                pltpu.make_async_copy(source.at[span], target.at[span], refs[2 * count].at[i * FETCHES + part])
            )
    for copy in copies:
        copy.start()
    for copy in copies:
        copy.wait()


def fetched(weights, held=()):
    count = len(weights)
    taken = sum(w.size * w.dtype.itemsize for w in (*weights, *held))
    spare = min(w.size * w.dtype.itemsize for w in weights) * 4 // 5
    return pl.pallas_call(
        functools.partial(fetch_kernel, count),
        out_shape=tuple(pltpu.VMEM(w.shape, w.dtype) for w in weights),
        in_specs=[pl.BlockSpec(memory_space=pl.ANY)] * count,
        out_specs=[pl.BlockSpec(memory_space=pltpu.VMEM)] * count,
        scratch_shapes=[pltpu.SemaphoreType.DMA((count * FETCHES,))],
        compiler_params=pltpu.CompilerParams(vmem_limit_bytes=VMEM_BYTES - taken - spare),
    )(*weights)


def share_kernel(own_ref, ids_ref, home_ref, gain_ref, router_ref, out_ref):
    rows, width = own_ref.shape
    experts = router_ref.shape[0]
    values = own_ref[...].astype(jnp.float32)
    meansq = jnp.mean(values * values, axis=-1, keepdims=True)
    normed = (values * lax.rsqrt(meansq + EPSILON) * gain_ref[...]).astype(jnp.bfloat16)
    logits = lax.dot_general(
        normed, router_ref[...], (((1,), (1,)), ((), ())), preferred_element_type=jnp.float32
    )
    affinity = jax.nn.sigmoid(logits)
    column = lax.broadcasted_iota(jnp.int32, (rows, experts), 1)
    named = jnp.zeros((rows, experts), jnp.bool_)
    for k in range(ids_ref.shape[1]):
        named = named | (ids_ref[:, k : k + 1] == column)
    chosen = jnp.where(named, affinity, 0.0)
    gates = chosen / jnp.sum(chosen, axis=1, keepdims=True)
    lane = lax.broadcasted_iota(jnp.int32, (rows, LANES), 1)
    extra = jnp.zeros((rows, LANES), jnp.float32)
    for k in range(experts):
        rest = jnp.sum(jnp.where(column == (home_ref[0] ^ k), gates, 0.0), axis=1, keepdims=True)
        for piece in range(PIECES):
            top = rest.astype(jnp.bfloat16).astype(jnp.float32)
            extra = jnp.where(lane == k * PIECES + piece, top, extra)
            rest = rest - top
    out_ref[:, :width] = own_ref[...]
    out_ref[:, width:] = extra.astype(jnp.bfloat16)


def with_shares(own, expert_ids, home, gain, router):
    rows, width = own.shape
    vmem = pl.BlockSpec(memory_space=pltpu.VMEM)
    return pl.pallas_call(
        share_kernel,
        out_shape=jax.ShapeDtypeStruct((rows, width + LANES), jnp.bfloat16),
        in_specs=[vmem, vmem, pl.BlockSpec(memory_space=pltpu.SMEM), vmem, vmem],
        out_specs=vmem,
        compiler_params=pltpu.CompilerParams(vmem_limit_bytes=4 << 20),
        name="shares",
    )(own, expert_ids, home, gain, router)


def fold_kernel(shards, *refs):
    outs = refs[shards:]
    rows = outs[0].shape[0]
    for k, out in enumerate(outs):
        span = pl.ds(k * rows, rows)
        total = refs[0][span, :].astype(jnp.float32)
        for part in refs[1:shards]:
            total = total + part[span, :].astype(jnp.float32)
        out[...] = total.astype(out.dtype)


def folded(parts, experts):
    rows, width = parts[0].shape[0] // experts, parts[0].shape[1]
    vmem = pl.BlockSpec(memory_space=pltpu.VMEM)
    return pl.pallas_call(
        functools.partial(fold_kernel, len(parts)),
        out_shape=tuple(
            jax.ShapeDtypeStruct((rows, width), jnp.float32 if k == 0 else jnp.bfloat16) for k in range(experts)
        ),
        in_specs=[vmem] * len(parts),
        out_specs=[vmem] * experts,
        compiler_params=pltpu.CompilerParams(vmem_limit_bytes=4 << 20),
        name="fold",
    )(*parts)


def finish_kernel(count, shared_ref, *refs):
    out_ref = refs[count]
    width = out_ref.shape[1]
    total = shared_ref[:, :width].astype(jnp.float32)
    extra = shared_ref[:, width:].astype(jnp.float32)
    lane = lax.broadcasted_iota(jnp.int32, extra.shape, 1)
    for k in range(count):
        terms = jnp.where((lane >= k * PIECES) & (lane < (k + 1) * PIECES), extra, 0.0)
        total = total + jnp.sum(terms, axis=1, keepdims=True) * refs[k][...].astype(jnp.float32)
    out_ref[...] = total.astype(jnp.bfloat16)


def finished(shared, pieces):
    rows, width = pieces[0].shape
    vmem = pl.BlockSpec(memory_space=pltpu.VMEM)
    return pl.pallas_call(
        functools.partial(finish_kernel, len(pieces)),
        out_shape=jax.ShapeDtypeStruct((rows, width), jnp.bfloat16),
        in_specs=[vmem] * (1 + len(pieces)),
        out_specs=vmem,
        compiler_params=pltpu.CompilerParams(vmem_limit_bytes=4 << 20),
        name="finish",
    )(shared, *pieces)


def expert_kernel(count, shards, *refs):
    blocks = refs[:count]
    gain_ref, gate_ref, lift_ref, down_ref = refs[count : count + 4]
    outs = refs[count + 4 : count + 4 + shards]
    normed_ref = refs[count + 4 + shards]
    rows = blocks[0].shape[0]
    gain = gain_ref[...]
    for pair in range(0, count, 2):
        parts = []
        for block in blocks[pair : pair + 2]:
            values = block[...].astype(jnp.float32)
            meansq = jnp.mean(values * values, axis=-1, keepdims=True)
            parts.append(values * lax.rsqrt(meansq + EPSILON) * gain)
        normed_ref[pl.ds(pair * rows, 2 * rows), :] = jnp.concatenate(parts, axis=0).astype(jnp.bfloat16)
    normed = normed_ref[...]
    gate_out = jnp.dot(normed, gate_ref[...], preferred_element_type=jnp.float32)
    lifted = jnp.dot(normed, lift_ref[...], preferred_element_type=jnp.float32)
    hidden = (gate_out / (1.0 + jnp.exp(-gate_out)) * lifted).astype(jnp.bfloat16)
    partial_value = jnp.dot(hidden, down_ref[...], preferred_element_type=jnp.float32).astype(jnp.bfloat16)
    share = partial_value.shape[0] // shards
    for i, out in enumerate(outs):
        out[...] = partial_value[i * share : (i + 1) * share]


def expert_parts(blocks, gain, gate, lift, down, shards):
    count = len(blocks)
    rows, width = blocks[0].shape
    return pl.pallas_call(
        functools.partial(expert_kernel, count, shards),
        out_shape=tuple(
            jax.ShapeDtypeStruct((count // shards * rows, width), jnp.bfloat16) for _ in range(shards)
        ),
        in_specs=[pl.BlockSpec(memory_space=pltpu.VMEM)] * (count + 4),
        out_specs=[pl.BlockSpec(memory_space=pltpu.VMEM)] * shards,
        scratch_shapes=[pltpu.VMEM((count * rows, width), jnp.bfloat16)],
        compiler_params=pltpu.CompilerParams(vmem_limit_bytes=8 << 20),
        name="experts",
    )(*blocks, gain, gate, lift, down)


def on_device(states, norm_gain, router, w_gate, w_up, w_down, routes):
    sections = lax.axis_size("section")
    devices = lax.axis_size("expert")
    experts = router.shape[2]
    shards = devices // experts
    send = functools.partial(relayed, sections=sections, experts=experts, shards=shards)
    far_first = range(experts - 1, 0, -1)

    def gathered(own):
        line = {0: own}
        for k in far_first:
            line[k] = send(own, hop=0, expert_bits=k, shard_bits=0)
        blocks = {(0, k): line[k] for k in range(experts)}
        for k in range(experts):
            for j in range(1, shards):
                blocks[j, k] = send(line[k], hop=0, expert_bits=0, shard_bits=j)
        return [blocks[j, k] for j in range(shards) for k in range(experts)]

    current = states[0]
    home = (lax.axis_index("expert") // shards).astype(jnp.int32)[None]
    matrices = (w_gate[0], w_up[0], w_down[0])
    for tick in range(TICKS):
        blocks = gathered(current)
        if tick == 0:
            early = fetched(matrices[:1])
            weights = (*early, *fetched(matrices[1:], matrices[:1]))
        parts = expert_parts(blocks, norm_gain, *weights, shards)
        arrived = []
        for j, part in enumerate(parts):
            arrived.append(send(part, hop=1, expert_bits=0, shard_bits=j))
        shared = with_shares(current, routes[tick, 0], home, norm_gain, router[0].T)
        shared = send(shared, hop=1, expert_bits=0, shard_bits=0)
        sums = folded(arrived, experts)
        pieces = {0: sums[0]}
        for k in far_first:
            pieces[k] = send(sums[k], hop=0, expert_bits=k, shard_bits=0)
        if tick + 1 < TICKS:
            weights = fetched(matrices)
        current = finished(shared, [pieces[k] for k in range(experts)])
    return current[None]


def solution(mesh):
    placed = (
        P("section", "expert", None),
        P("section", None),
        P("section", None, None),
        P("section", None, "expert"),
        P("section", None, "expert"),
        P("section", "expert", None),
        P(None, "section", "expert", None),
    )
    return jax.shard_map(
        on_device,
        mesh=mesh,
        in_specs=placed,
        out_specs=P("section", "expert", None),
        check_vma=False,
    )
```
